32 devices in a mesh: groups: 2 (over y), tensor: 4 (over z), dp: 4 (over x, core).
Axes of the slice: x: 2, y: 2, z: 4, core: 2. Of those that a mesh axis runs over, the one named last changes fastest.
Arguments:
- root_features: bfloat16 [32, 16384], P('groups', 'dp'), parts along dimension 0, may hold values from -6 to 6
- branch_embeds: bfloat16 [32, 4, 8, 16384], P('groups', None, None, 'dp'), parts along dimension 0, may hold values from -6 to 6
- parents: int32 [32, 3, 8], P('groups'), parts along dimension 0, may hold values from 0 to 7
- cache_lengths: int32 [32], P(('groups', 'dp')), parts along dimension 0, may hold values from 128 to 512, as said below
- cache_kv: bfloat16 [32, 2, 512, 512], P(('groups', 'dp'), None, None, 'tensor'), parts along dimension 0, may hold values from -6 to 6, as said below
- norm_gain: bfloat16 [16384], P('dp'), may hold values from 0.099609375 to 1.8984375
- w_query: bfloat16 [16384, 2048], P('dp', 'tensor'), may hold values from -1 to 1
- w_keyval: bfloat16 [16384, 2, 512], P('dp', None, 'tensor'), may hold values from -1 to 1, as said below
- w_out: bfloat16 [2048, 16384], P('tensor', 'dp'), may hold values from -0.125 to 0.125
Outputs:
- tree_features: bfloat16 [32, 4, 8, 16384], P('groups', None, None, ('dp', 'tensor')), parts along dimension 0
The draws below stay inside these ranges and needn't reach their ends.
There are 2 independent parts, one for each index of `groups`. The reference program is written for one: setup_inputs(seed, part) draws one part's arguments, and reference() takes and returns one part's arrays. A program takes and returns all parts, laid end to end along the dimension named above; an argument that names none is the same for every part. Nothing has to cross between parts.
Inputs may be any that keep to these rules, and one draw needn't show every extreme that they name: `cache_lengths`: some request has exactly 512 valid cache positions and some other exactly 128. `cache_kv`: for each request, keys and values, the 4 blocks of 128 columns k * 4 .. (k + 1) * 4 - 1 are equal; they hold key-value head k. `w_keyval`: for keys and values, the 4 blocks of 128 columns k * 4 .. (k + 1) * 4 - 1 are equal; they hold key-value head k.
All inputs are finite; a program needn't handle non-finite values.
Results may differ from the reference program's by a relative error of at most 0.017.
Values may be sent and summed in bfloat16 or wider, within the bound.
A program may use at most 128 MiB of HBM per device.

```python
import jax
import jax.numpy as jnp
from jax import lax

D = 16384
HD = 128
HEADS_DEV = 4
BRANCH = 8
DEPTHS = 4
CACHE = 512
REQUESTS = 16
HEADS = 16
KV = 1
COPIES = 4
N_TENSOR = 4


def draw_cache_lengths(key, part):
    first, second, third = jax.random.split(jax.random.fold_in(key, 17), 3)
    lengths = jax.random.randint(first, (REQUESTS,), CACHE // 4, CACHE + 1, dtype=jnp.int32)
    longest = jax.random.randint(second, (), 0, REQUESTS, dtype=jnp.int32)
    offset = jax.random.randint(third, (), 1, REQUESTS, dtype=jnp.int32)
    shortest = (longest + offset) % REQUESTS
    index_row = jnp.arange(REQUESTS, dtype=jnp.int32)
    lengths = jnp.where(index_row == shortest, CACHE // 4, lengths)
    return jnp.where(index_row == longest, CACHE, lengths).astype(jnp.int32)


def draw_cache_kv(key, part):
    entries = jax.random.normal(jax.random.fold_in(key, 37), (REQUESTS, 2, CACHE, KV, 1, HD), jnp.float32)
    entries = jnp.clip(entries, -6.0, 6.0)
    copied = jnp.broadcast_to(entries, (REQUESTS, 2, CACHE, KV, COPIES, HD))
    return copied.reshape(REQUESTS, 2, CACHE, KV * COPIES * HD).astype(jnp.bfloat16)


def shared_blocks(key):
    key_seed, value_seed = jax.random.split(jax.random.fold_in(key, 29), 2)
    key_block = jnp.clip(jax.random.normal(key_seed, (D, KV, HD), jnp.float32), -6.0, 6.0)
    value_block = jnp.clip(jax.random.normal(value_seed, (D, KV, HD), jnp.float32), -6.0, 6.0)
    return (key_block, value_block)


def draw_w_keyval(key, part):
    key_block, value_block = shared_blocks(key)
    stacked = jnp.stack([key_block, value_block], axis=1) * D ** (-0.5)
    copied = jnp.broadcast_to(stacked[:, :, :, None, :], (D, 2, KV, COPIES, HD))
    return jnp.clip(copied, -1.0, 1.0).reshape(D, 2, KV * COPIES * HD).astype(jnp.bfloat16)


def draw_w_query(key, part):
    base_seed = jax.random.fold_in(jax.random.fold_in(key, 31), 0)
    total = jnp.clip(jax.random.normal(base_seed, (D, HEADS, HD), jnp.float32), -6.0, 6.0)
    return jnp.clip(total * D ** (-0.5), -1.0, 1.0).reshape(D, HEADS * HD).astype(jnp.bfloat16)


def touch_ends(values, key, smallest, top_value):
    spot = [jax.random.randint(jax.random.fold_in(key, axis), (), 0, length) for axis, length in enumerate(values.shape)]
    widest = values.shape.index(max(values.shape))
    neighbour = spot[:widest] + [(spot[widest] + 1) % values.shape[widest]] + spot[widest + 1:]
    return values.at[tuple(spot)].set(smallest).at[tuple(neighbour)].set(top_value)


def levels(key, shape, pieces, smallest, high):
    def one(position, shards_of):
        steps = jax.random.uniform(jax.random.fold_in(jax.random.fold_in(key, 6), position), (shards_of,), jnp.float32, smallest / len(pieces), high / len(pieces))
        return jnp.repeat(jnp.exp(steps), shape[position] // shards_of).reshape((-1,) + (1,) * (len(shape) - position - 1))

    level = one(*pieces[0])
    for cut in pieces[1:]:
        level = level * one(*cut)
    return level


def gaussian(own_key, extent, spread, reach, pieces=(), held_as=jnp.bfloat16):
    factor_of = levels(own_key, extent, pieces, -0.22, 0.18) if pieces else 1.0
    array = jax.random.normal(own_key, extent, jnp.float32) * spread * factor_of
    return jnp.minimum(jnp.maximum(array, -reach), reach).astype(held_as)


def setup_inputs(seed: int = 0, part: int = 0) -> dict:
    arg_keys = jax.random.split(jax.random.key(seed), 10)
    part_keys = jax.random.split(jax.random.fold_in(arg_keys[9], part), 10)
    return {
        "root_features": gaussian(part_keys[0], (REQUESTS, D), 1.0, 6.0, ((1, 4),)),
        "branch_embeds": gaussian(part_keys[1], (REQUESTS, DEPTHS, BRANCH, D), 1.0, 6.0, ((3, 4),)),
        "parents": touch_ends(jax.random.randint(part_keys[2], (REQUESTS, DEPTHS - 1, BRANCH), 0, BRANCH), jax.random.fold_in(part_keys[2], 1), 0, BRANCH - 1).astype(jnp.int32),
        "cache_lengths": draw_cache_lengths(jax.random.fold_in(jax.random.fold_in(arg_keys[9], part), 71), part),
        "cache_kv": draw_cache_kv(jax.random.fold_in(jax.random.fold_in(arg_keys[9], part), 71), part),
        "norm_gain": jnp.clip(1.0 + 0.18 * jax.random.normal(arg_keys[5], (D,), jnp.float32), 0.099609375, 1.8984375).astype(jnp.bfloat16),
        "w_query": draw_w_query(jax.random.fold_in(arg_keys[9], 71), part),
        "w_keyval": draw_w_keyval(jax.random.fold_in(arg_keys[9], 71), part),
        "w_out": gaussian(arg_keys[8], (HEADS * HD, D), (HEADS * HD) ** -0.5, 0.125, ((0, 4), (1, 4))),
    }


epsilon = 1e-05
masked_score = -1e+30

def ancestor_path(parent_table, tree_level):
    current = jnp.broadcast_to(jnp.arange(BRANCH, dtype=jnp.int32)[None, :], (parent_table.shape[0], BRANCH))
    path_nodes = [current]
    for upper in range(tree_level, 0, -1):
        current = jnp.take_along_axis(parent_table[:, upper - 1], current, axis=1)
        path_nodes.append(current)
    return path_nodes[::-1]

def tree_mask_of(parent_table, tree_level):
    path_nodes = ancestor_path(parent_table, tree_level)
    columns = jnp.arange(BRANCH, dtype=jnp.int32)
    blocks = []
    for other_level in range(DEPTHS):
        if other_level <= tree_level:
            blocks.append(columns[None, None, :] == path_nodes[other_level][:, :, None])
        else:
            blocks.append(jnp.zeros((parent_table.shape[0], BRANCH, BRANCH), dtype=bool))
    return jnp.concatenate(blocks, axis=2)

def attend_one(packed):
    queries, cache_keys, cache_values, tree_keys, tree_values, cache_valid, tree_mask = packed
    kv_heads = cache_keys.shape[1]
    grouped = queries.astype(jnp.float32).reshape(BRANCH, kv_heads, -1, HD)
    cache_scores = jnp.einsum('bkgd,ckd->kgbc', grouped, cache_keys.astype(jnp.float32)) * HD ** (-0.5)
    tree_scores = jnp.einsum('bkgd,tkd->kgbt', grouped, tree_keys.astype(jnp.float32)) * HD ** (-0.5)
    cache_scores = jnp.where(cache_valid[None, None, None, :], cache_scores, masked_score)
    tree_scores = jnp.where(tree_mask[None, None, :, :], tree_scores, masked_score)
    row_max = jnp.maximum(lax.optimization_barrier(jnp.max(cache_scores, axis=3)), lax.optimization_barrier(jnp.max(tree_scores, axis=3)))[..., None]
    cache_exp = jnp.exp(cache_scores - row_max)
    tree_exp = jnp.exp(tree_scores - row_max)
    denominator = lax.optimization_barrier(jnp.sum(cache_exp, axis=3, keepdims=True)) + lax.optimization_barrier(jnp.sum(tree_exp, axis=3, keepdims=True))
    cache_weights = (cache_exp / denominator).astype(jnp.bfloat16)
    tree_weights = (tree_exp / denominator).astype(jnp.bfloat16)
    mixed = jnp.einsum('kgbc,ckd->bkgd', cache_weights.astype(jnp.float32), cache_values.astype(jnp.float32))
    mixed = mixed + jnp.einsum('kgbt,tkd->bkgd', tree_weights.astype(jnp.float32), tree_values.astype(jnp.float32))
    return mixed.reshape(BRANCH, -1).astype(jnp.bfloat16)

def reference(root_features, branch_embeds, parents, cache_lengths, cache_kv, norm_gain, w_query, w_keyval, w_out):
    request_count = root_features.shape[0]
    kv_heads = KV
    kv_cols = kv_heads * HD
    all_rows = request_count * BRANCH
    first_copy = cache_kv.reshape(request_count, 2, CACHE, kv_heads, COPIES, HD)[:, :, :, :, 0]
    cache_keys = first_copy[:, 0]
    cache_values = first_copy[:, 1]
    positions = jnp.arange(CACHE, dtype=jnp.int32)
    cache_valid = positions[None, :] < cache_lengths[:, None]
    tree_keys = jnp.zeros((request_count, DEPTHS * BRANCH, kv_heads, HD), jnp.bfloat16)
    tree_values = jnp.zeros((request_count, DEPTHS * BRANCH, kv_heads, HD), jnp.bfloat16)
    keyval_weight = w_keyval.reshape(D, 2, kv_heads, COPIES, HD)[:, :, :, 0].reshape(D, 2 * kv_cols)
    out_blocks = w_out.reshape(N_TENSOR, HEADS_DEV * HD, D)
    gain = norm_gain.astype(jnp.float32)
    results = []
    previous = None
    for tree_level in range(DEPTHS):
        if tree_level == 0:
            parent = jnp.broadcast_to(root_features[:, None, :], (request_count, BRANCH, D))
        else:
            parent = jnp.take_along_axis(previous, parents[:, tree_level - 1][:, :, None], axis=1)
        node_state = parent.astype(jnp.float32) + branch_embeds[:, tree_level].astype(jnp.float32)
        flat_state = node_state.reshape(all_rows, D)
        inv_rms = lax.rsqrt(lax.optimization_barrier(jnp.mean(flat_state * flat_state, axis=1, keepdims=True)) + epsilon)
        scaled = (flat_state * gain).astype(jnp.bfloat16)
        queries = (jnp.dot(scaled, w_query, preferred_element_type=jnp.float32) * inv_rms).astype(jnp.bfloat16)
        keyval = (jnp.dot(scaled, keyval_weight, preferred_element_type=jnp.float32) * inv_rms).astype(jnp.bfloat16)
        new_keys = keyval[:, :kv_cols].reshape(request_count, BRANCH, kv_heads, HD)
        new_values = keyval[:, kv_cols:].reshape(request_count, BRANCH, kv_heads, HD)
        tree_keys = tree_keys.at[:, tree_level * BRANCH:(tree_level + 1) * BRANCH].set(new_keys)
        tree_values = tree_values.at[:, tree_level * BRANCH:(tree_level + 1) * BRANCH].set(new_values)
        tree_mask = tree_mask_of(parents, tree_level)
        attended = lax.map(attend_one, (queries.reshape(request_count, BRANCH, -1), cache_keys, cache_values, tree_keys, tree_values, cache_valid, tree_mask))
        head_groups = jnp.swapaxes(attended.reshape(all_rows, N_TENSOR, HEADS_DEV * HD), 0, 1)

        def add_group(carry, pair):
            group_rows, group_weight = pair
            partial_sum = jnp.dot(group_rows, group_weight, preferred_element_type=jnp.float32).astype(jnp.bfloat16)
            partial_sum = lax.optimization_barrier(partial_sum)
            return (carry + partial_sum.astype(jnp.float32), None)
        summed, _ = lax.scan(add_group, jnp.zeros((all_rows, D), jnp.float32), (head_groups, out_blocks))
        fresh = (flat_state + summed).astype(jnp.bfloat16).reshape(request_count, BRANCH, D)
        results.append(fresh)
        previous = fresh
    return jnp.stack(results, axis=1)
```

```python
import functools

import jax
import jax.numpy as jnp
from jax import lax
from jax.experimental import pallas as pl
from jax.experimental.pallas import tpu as pltpu
from jax.sharding import PartitionSpec as P

D = 16384
HD = 128
BRANCH = 8
DEPTHS = 4
CACHE = 512


epsilon = 1e-05
masked_score = -1e30


def ancestor_path(parent_table, tree_level):
    current = jnp.broadcast_to(
        jnp.arange(BRANCH, dtype=jnp.int32)[None, :], (parent_table.shape[0], BRANCH)
    )
    path_nodes = [current]
    for upper in range(tree_level, 0, -1):
        current = jnp.take_along_axis(parent_table[:, upper - 1], current, axis=1)
        path_nodes.append(current)
    return path_nodes[::-1]


def tree_mask_of(parent_table, tree_level):
    path_nodes = ancestor_path(parent_table, tree_level)
    columns = jnp.arange(BRANCH, dtype=jnp.int32)
    blocks = []
    for other_level in range(DEPTHS):
        if other_level <= tree_level:
            blocks.append(columns[None, None, :] == path_nodes[other_level][:, :, None])
        else:
            blocks.append(jnp.zeros((parent_table.shape[0], BRANCH, BRANCH), dtype=bool))
    return jnp.concatenate(blocks, axis=2)


def shards(
    root_features,
    branch_embeds,
    parents,
    cache_lengths,
    cache_kv,
    norm_gain,
    w_query,
    w_keyval,
    w_out,
):
    request_count, feat_cols = root_features.shape
    local_requests = cache_lengths.shape[0]
    head_cols = w_query.shape[1]
    kv_cols = w_keyval.shape[2]
    kv_local = kv_cols // HD
    all_rows = request_count * BRANCH
    own_rows = local_requests * BRANCH
    share_cols = feat_cols // lax.axis_size("tensor")
    dp_index = lax.axis_index("dp")
    tensor_index = lax.axis_index("tensor")
    weights = jnp.concatenate([w_query, w_keyval.reshape(feat_cols, 2 * kv_cols)], axis=1)
    gain = norm_gain.astype(jnp.float32)
    own_parents = lax.dynamic_slice_in_dim(parents, dp_index * local_requests, local_requests, 0)
    cache_keys = cache_kv[:, 0].reshape(local_requests, CACHE, kv_local, HD)
    cache_values = cache_kv[:, 1].reshape(local_requests, CACHE, kv_local, HD)
    positions = jnp.arange(CACHE, dtype=jnp.int32)
    cache_valid = positions[None, :] < cache_lengths[:, None]
    tree_keys = jnp.zeros((local_requests, DEPTHS * BRANCH, kv_local, HD), jnp.bfloat16)
    tree_values = jnp.zeros((local_requests, DEPTHS * BRANCH, kv_local, HD), jnp.bfloat16)
    results = []
    previous = None
    for tree_level in range(DEPTHS):
        if tree_level == 0:
            parent = jnp.broadcast_to(root_features[:, None, :], (request_count, BRANCH, feat_cols))
        else:
            parent = jnp.take_along_axis(previous, parents[:, tree_level - 1][:, :, None], axis=1)
        node_state = parent.astype(jnp.float32) + branch_embeds[:, tree_level].astype(jnp.float32)
        flat_state = node_state.reshape(all_rows, feat_cols)
        square_sums = jnp.sum(flat_state * flat_state, axis=1)
        scaled = (flat_state * gain).astype(jnp.bfloat16)
        total_sums = lax.psum(square_sums, "dp")
        own_sums = lax.dynamic_slice_in_dim(total_sums, dp_index * own_rows, own_rows, 0)
        proj_terms = lax.psum_scatter(
            jnp.dot(scaled, weights, preferred_element_type=jnp.float32).astype(jnp.bfloat16),
            "dp",
            scatter_dimension=0,
            tiled=True,
        ).astype(jnp.float32)
        inv_rms = lax.rsqrt(own_sums / D + epsilon)[:, None]
        projected = (proj_terms * inv_rms).astype(jnp.bfloat16)
        queries = projected[:, :head_cols].reshape(local_requests, BRANCH, kv_local, -1, HD)
        new_keys = projected[:, head_cols : head_cols + kv_cols].reshape(
            local_requests, BRANCH, kv_local, HD
        )
        new_values = projected[:, head_cols + kv_cols :].reshape(
            local_requests, BRANCH, kv_local, HD
        )
        tree_keys = tree_keys.at[:, tree_level * BRANCH : (tree_level + 1) * BRANCH].set(new_keys)
        tree_values = tree_values.at[:, tree_level * BRANCH : (tree_level + 1) * BRANCH].set(
            new_values
        )
        tree_mask = tree_mask_of(own_parents, tree_level)
        cache_scores = jnp.einsum(
            "rbkgd,rckd->rkgbc", queries, cache_keys, preferred_element_type=jnp.float32
        ) * HD ** (-0.5)
        tree_scores = jnp.einsum(
            "rbkgd,rtkd->rkgbt", queries, tree_keys, preferred_element_type=jnp.float32
        ) * HD ** (-0.5)
        cache_scores = jnp.where(cache_valid[:, None, None, None, :], cache_scores, masked_score)
        tree_scores = jnp.where(tree_mask[:, None, None, :, :], tree_scores, masked_score)
        row_max = jnp.maximum(jnp.max(cache_scores, axis=4), jnp.max(tree_scores, axis=4))[
            ..., None
        ]
        cache_exp = jnp.exp(cache_scores - row_max)
        tree_exp = jnp.exp(tree_scores - row_max)
        denominator = jnp.sum(cache_exp, axis=4, keepdims=True) + jnp.sum(
            tree_exp, axis=4, keepdims=True
        )
        cache_weights = (cache_exp / denominator).astype(jnp.bfloat16)
        tree_weights = (tree_exp / denominator).astype(jnp.bfloat16)
        mixed = jnp.einsum(
            "rkgbc,rckd->rbkgd", cache_weights, cache_values, preferred_element_type=jnp.float32
        )
        mixed = mixed + jnp.einsum(
            "rkgbt,rtkd->rbkgd", tree_weights, tree_values, preferred_element_type=jnp.float32
        )
        attended = mixed.reshape(own_rows, head_cols).astype(jnp.bfloat16)
        partial_out = jnp.dot(
            lax.all_gather(attended, "dp", axis=0, tiled=True),
            w_out,
            preferred_element_type=jnp.float32,
        )
        share_sums = lax.psum_scatter(
            partial_out.astype(jnp.bfloat16), "tensor", scatter_dimension=1, tiled=True
        ).astype(jnp.float32)
        residual = lax.dynamic_slice_in_dim(flat_state, tensor_index * share_cols, share_cols, 1)
        fresh_share = (residual + share_sums).astype(jnp.bfloat16)
        if tree_level + 1 < DEPTHS:
            gathered = lax.all_gather(fresh_share, "tensor", axis=1, tiled=True)
            previous = gathered.reshape(request_count, BRANCH, feat_cols)
        results.append(fresh_share.reshape(request_count, BRANCH, share_cols))
    return jnp.stack(results, axis=1)


MESH = pl.DeviceIdType.MESH


def dot32(a, b):
    return jnp.dot(a, b, preferred_element_type=jnp.float32)


def dot32_t(a, b):
    return lax.dot_general(a, b, (((1,), (1,)), ((), ())), preferred_element_type=jnp.float32)


def tree_kernel(
    n,
    m,
    root_ref,
    emb_hbm,
    hot_ref,
    own_hot_ref,
    len_ref,
    cache_hbm,
    gain_ref,
    wq_hbm,
    wkv_hbm,
    wo_hbm,
    out_ref,
    emb0,
    emb_share,
    cache,
    wq,
    wkv,
    wo,
    scaled,
    share_sums,
    state,
    proj,
    proj_send,
    proj_recv,
    sums_send,
    sums_recv,
    tree_keys,
    tree_values,
    tree_mask,
    att,
    part,
    rs_send,
    rs_recv,
    total,
    load_sem,
    ag_ssem,
    ag_rsem,
    tsum_ssem,
    tsum_rsem,
    proj_ssem,
    proj_rsem,
    dsum_ssem,
    dsum_rsem,
    att_ssem,
    att_rsem,
    rs_ssem,
    rs_rsem,
):
    t = lax.axis_index("tensor")
    d = lax.axis_index("dp")
    requests, feat = root_ref.shape
    rows = requests * BRANCH
    own = rows // m
    own_requests = requests // m
    share = feat // n
    head_cols = wq.shape[1]
    heads = head_cols // HD

    def cols_of(s):
        return pl.ds(pl.multiple_of(s * share, share), share)

    loads = [
        pltpu.make_async_copy(emb_hbm.at[:, 0], emb0, load_sem.at[0]),
        pltpu.make_async_copy(wq_hbm, wq, load_sem.at[1]),
        pltpu.make_async_copy(wkv_hbm, wkv, load_sem.at[2]),
        pltpu.make_async_copy(cache_hbm, cache, load_sem.at[3]),
        pltpu.make_async_copy(wo_hbm, wo, load_sem.at[4]),
    ]
    for e in range(1, DEPTHS):
        loads.append(
            pltpu.make_async_copy(
                emb_hbm.at[:, e, :, cols_of(t)], emb_share.at[e - 1], load_sem.at[4 + e]
            )
        )
    for load in loads:
        load.start()

    dp_to = [lax.rem(d + k, m) for k in range(1, m)]
    t_to = [lax.rem(t + k, n) for k in range(1, n)]

    barrier = pltpu.get_barrier_semaphore()
    for peer in dp_to:
        pl.semaphore_signal(barrier, inc=1, device_id={"dp": peer}, device_id_type=MESH)
    for peer in t_to:
        pl.semaphore_signal(barrier, inc=1, device_id={"tensor": peer}, device_id_type=MESH)
    pl.semaphore_wait(barrier, m + n - 2)

    def ag_copy(e, s, to, send_slot):
        return pltpu.make_async_remote_copy(
            src_ref=scaled.at[e, s],
            dst_ref=scaled.at[e, s],
            send_sem=ag_ssem.at[e, send_slot],
            recv_sem=ag_rsem.at[e, s],
            device_id={"tensor": to},
            device_id_type=MESH,
        )

    def tsum_copy(e, k):
        return pltpu.make_async_remote_copy(
            src_ref=share_sums.at[e, n - 1],
            dst_ref=share_sums.at[e, k],
            send_sem=tsum_ssem.at[e, k],
            recv_sem=tsum_rsem.at[e, k],
            device_id={"tensor": t_to[k]},
            device_id_type=MESH,
        )

    def proj_copy(e, k):
        return pltpu.make_async_remote_copy(
            src_ref=proj_send.at[e, dp_to[k]],
            dst_ref=proj_recv.at[e, k],
            send_sem=proj_ssem.at[e, k],
            recv_sem=proj_rsem.at[e, k],
            device_id={"dp": dp_to[k]},
            device_id_type=MESH,
        )

    def dsum_copy(e, k):
        return pltpu.make_async_remote_copy(
            src_ref=sums_send.at[e],
            dst_ref=sums_recv.at[e, k],
            send_sem=dsum_ssem.at[e, k],
            recv_sem=dsum_rsem.at[e, k],
            device_id={"dp": dp_to[k]},
            device_id_type=MESH,
        )

    def att_copy(e, k):
        return pltpu.make_async_remote_copy(
            src_ref=att.at[e, d],
            dst_ref=att.at[e, d],
            send_sem=att_ssem.at[e, k],
            recv_sem=att_rsem.at[e, k],
            device_id={"dp": dp_to[k]},
            device_id_type=MESH,
        )

    def rs_copy(e, s, to, slot):
        return pltpu.make_async_remote_copy(
            src_ref=rs_send.at[e, s],
            dst_ref=rs_recv.at[e, slot],
            send_sem=rs_ssem.at[e, s],
            recv_sem=rs_rsem.at[e, slot],
            device_id={"tensor": to},
            device_id_type=MESH,
        )

    def rs_right(e, s):
        return rs_copy(e, s, t + 1, s)

    def rs_left(e, s):
        return rs_copy(e, s, t - 1, jnp.where(t - 1 == s, n, s))

    def rs_wait(e, slot):
        rs_copy(e, 0, lax.rem(t + 1, n), slot).wait_recv()

    row_id = lax.broadcasted_iota(jnp.int32, (rows, rows), 0)
    col_id = lax.broadcasted_iota(jnp.int32, (rows, rows), 1)
    eye = row_id == col_id

    def to_lanes(column):
        spread = jnp.where(eye, jnp.broadcast_to(column, (rows, rows)), 0.0)
        return jnp.broadcast_to(jnp.sum(spread, axis=0, keepdims=True), (8, rows))

    spread_id = lax.broadcasted_iota(jnp.int32, (rows, requests), 0) // BRANCH
    root_hot = (
        spread_id == lax.broadcasted_iota(jnp.int32, (rows, requests), 1)
    ).astype(jnp.bfloat16)
    loads[0].wait()
    squares = jnp.zeros((rows, 1), jnp.float32)
    for s in range(n):
        cols = slice(s * share, (s + 1) * share)
        node = dot32(root_hot, root_ref[:, cols]) + emb0[:, :, cols].astype(jnp.float32).reshape(
            rows, share
        )
        squares = squares + jnp.sum(node * node, axis=1, keepdims=True)
        scaled[0, s] = (node * gain_ref[:, cols]).astype(jnp.bfloat16)

        @pl.when(t == s)
        def _():
            state[...] = node

    sums_send[0] = to_lanes(squares)
    tree_keys[...] = jnp.zeros_like(tree_keys)
    tree_values[...] = jnp.zeros_like(tree_values)
    tree_mask[...] = jnp.zeros_like(tree_mask)
    for load in loads[1:]:
        load.wait()

    def level(e, carry):
        def product(s):
            block = scaled[e, s]
            proj[:, :head_cols] += dot32(block, wq[cols_of(s)])
            proj[:, head_cols:] += dot32(block, wkv[cols_of(s)])

        proj[...] = jnp.zeros_like(proj)
        product(t)

        for k in range(1, n):
            before = t - k
            after = t + k

            @pl.when((before >= 0) & (e > 0))
            def _():
                ag_copy(e, before, lax.rem(t + 1, n), before).wait_recv()

                @pl.when(t < n - 1)
                def _():
                    ag_copy(e, before, t + 1, before).start()

            @pl.when((after < n) & (e > 0))
            def _():
                ag_copy(e, after, lax.rem(t + 1, n), after).wait_recv()

                @pl.when(t > 0)
                def _():
                    ag_copy(e, after, t - 1, after).start()

            @pl.when(before >= 0)
            def _():
                product(before)

            @pl.when(after < n)
            def _():
                product(after)

        @pl.when(e > 0)
        def _():
            summed = share_sums[e, n - 1]
            for k in range(n - 1):
                tsum_copy(e, k).wait_recv()
                summed = summed + share_sums[e, k]
            sums_send[e] = summed

        for k in range(m):
            proj_send[e, k] = proj[k * own : (k + 1) * own].astype(jnp.bfloat16)
        for k in range(m - 1):
            proj_copy(e, k).start()
            dsum_copy(e, k).start()

        own_row = lax.broadcasted_iota(jnp.int32, (own, DEPTHS * own), 0)
        own_col = lax.broadcasted_iota(jnp.int32, (own, DEPTHS * own), 1)
        itself = (own_col == own_row + e * own).astype(jnp.float32)
        above = dot32(own_hot_ref[e], tree_mask[...])
        mask_now = itself + above
        tree_mask[...] = mask_now.astype(jnp.bfloat16)

        projected = proj[pl.ds(pl.multiple_of(d * own, own), own)]
        summed = sums_send[e]
        for k in range(m - 1):
            proj_copy(e, k).wait_recv()
            dsum_copy(e, k).wait_recv()
            projected = projected + proj_recv[e, k].astype(jnp.float32)
            summed = summed + sums_recv[e, k]
        pick = lax.broadcasted_iota(jnp.int32, (own, rows), 1) == (
            lax.broadcasted_iota(jnp.int32, (own, rows), 0) + d * own
        )
        own_sums = jnp.sum(
            jnp.where(pick, jnp.broadcast_to(summed[0:1], (own, rows)), 0.0),
            axis=1,
            keepdims=True,
        )
        inv_rms = lax.rsqrt(own_sums / (feat * m) + epsilon)
        projected = projected * inv_rms
        queries = jnp.concatenate(
            [
                projected[:, h * HD : (h + 1) * HD].reshape(own_requests, 1, BRANCH, HD)
                for h in range(heads)
            ],
            axis=1,
        ).reshape(own * heads, HD).astype(jnp.bfloat16)
        now = pl.ds(pl.multiple_of(e * own, own), own)
        tree_keys[now] = projected[:, head_cols : head_cols + HD].astype(jnp.bfloat16)
        tree_values[now] = projected[:, head_cols + HD :].astype(jnp.bfloat16)

        per = heads * BRANCH
        tree_scores = dot32_t(queries, tree_keys[...]) * HD ** (-0.5)
        allowed = jnp.broadcast_to(
            mask_now.reshape(own_requests, 1, BRANCH, DEPTHS * own),
            (own_requests, heads, BRANCH, DEPTHS * own),
        ).reshape(own * heads, DEPTHS * own)
        tree_scores = jnp.where(allowed > 0.5, tree_scores, masked_score)
        cache_scores = []
        position = lax.broadcasted_iota(jnp.int32, (per, CACHE), 1)
        for r in range(own_requests):
            scores = dot32_t(queries[r * per : (r + 1) * per], cache[r, 0]) * HD ** (-0.5)
            cache_scores.append(jnp.where(position < len_ref[r], scores, masked_score))
        cache_scores = jnp.concatenate(cache_scores, axis=0)
        row_max = jnp.maximum(
            jnp.max(cache_scores, axis=1, keepdims=True),
            jnp.max(tree_scores, axis=1, keepdims=True),
        )
        cache_exp = jnp.exp(cache_scores - row_max)
        tree_exp = jnp.exp(tree_scores - row_max)
        denominator = jnp.sum(cache_exp, axis=1, keepdims=True) + jnp.sum(
            tree_exp, axis=1, keepdims=True
        )
        cache_weights = (cache_exp / denominator).astype(jnp.bfloat16)
        tree_weights = (tree_exp / denominator).astype(jnp.bfloat16)
        mixed = jnp.concatenate(
            [
                dot32(cache_weights[r * per : (r + 1) * per], cache[r, 1])
                for r in range(own_requests)
            ],
            axis=0,
        ) + dot32(tree_weights, tree_values[...])
        mixed = mixed.reshape(own_requests, heads, BRANCH, HD)
        for h in range(heads):
            att[e, d, :, h * HD : (h + 1) * HD] = mixed[:, h].reshape(own, HD).astype(jnp.bfloat16)
        for k in range(m - 1):
            att_copy(e, k).start()
        for k in range(m - 1):
            att_copy(e, k).wait_recv()

        attended = att[e].reshape(rows, head_cols)

        def own_part(s):
            part[s] = dot32(attended, wo[:, s * share : (s + 1) * share])

        done = set()
        for k in range(n - 1):
            right, left = n - 1 - k, k
            for s in (right, left):
                if s not in done:
                    own_part(s)
                    done.add(s)

            @pl.when(t == 0)
            def _():
                rs_send[e, right] = part[right].astype(jnp.bfloat16)
                rs_right(e, right).start()

            @pl.when(t == n - 1)
            def _():
                rs_send[e, left] = part[left].astype(jnp.bfloat16)
                rs_left(e, left).start()

        def relay_right(s):
            @pl.when((t > 0) & (t < s))
            def _():
                rs_wait(e, s)
                rs_send[e, s] = (part[s] + rs_recv[e, s].astype(jnp.float32)).astype(jnp.bfloat16)
                rs_right(e, s).start()

        def relay_left(s):
            @pl.when((t < n - 1) & (t > s))
            def _():
                rs_wait(e, s)
                rs_send[e, s] = (part[s] + rs_recv[e, s].astype(jnp.float32)).astype(jnp.bfloat16)
                rs_left(e, s).start()

        @pl.when(t < n // 2)
        def _():
            for k in range(n - 1):
                relay_right(n - 1 - k)
                relay_left(k)

        @pl.when(t >= n // 2)
        def _():
            for k in range(n - 1):
                relay_left(k)
                relay_right(n - 1 - k)

        total[...] = state[...] + part[t]

        @pl.when(t > 0)
        def _():
            rs_wait(e, t)
            total[...] += rs_recv[e, t].astype(jnp.float32)

        @pl.when(t < n - 1)
        def _():
            rs_wait(e, n)
            total[...] += rs_recv[e, n].astype(jnp.float32)

        fresh = total[...]
        out_ref[:, pl.ds(e, 1)] = fresh.reshape(requests, 1, BRANCH, share).astype(jnp.bfloat16)

        @pl.when(e < DEPTHS - 1)
        def _():
            node = dot32(hot_ref[e], fresh.astype(jnp.bfloat16)) + emb_share[e].astype(
                jnp.float32
            ).reshape(rows, share)
            state[...] = node
            scaled[e + 1, t] = (node * gain_ref[:, cols_of(t)]).astype(jnp.bfloat16)

            @pl.when(t < n - 1)
            def _():
                ag_copy(e + 1, t, t + 1, t).start()

            @pl.when(t > 0)
            def _():
                ag_copy(e + 1, t, t - 1, n).start()

            share_sums[e + 1, n - 1] = to_lanes(jnp.sum(node * node, axis=1, keepdims=True))
            for k in range(n - 1):
                tsum_copy(e + 1, k).start()

        return carry

    lax.fori_loop(0, DEPTHS, level, 0)

    def drain(e, carry):
        for k in range(m - 1):
            proj_copy(e, k).wait_send()
            dsum_copy(e, k).wait_send()
            att_copy(e, k).wait_send()
        for s in range(n):

            @pl.when(t < s)
            def _():
                rs_right(e, s).wait_send()

            @pl.when(t > s)
            def _():
                rs_left(e, s).wait_send()

        @pl.when(e > 0)
        def _():
            for k in range(n - 1):
                tsum_copy(e, k).wait_send()
            for s in range(n):

                @pl.when((s <= t) & (t < n - 1))
                def _():
                    ag_copy(e, s, t + 1, s).wait_send()

                @pl.when((s > t) & (t > 0))
                def _():
                    ag_copy(e, s, t - 1, s).wait_send()

            @pl.when(t > 0)
            def _():
                ag_copy(e, t, t - 1, n).wait_send()

        return carry

    lax.fori_loop(0, DEPTHS, drain, 0)


def kernel_shards(
    root_features,
    branch_embeds,
    parents,
    cache_lengths,
    cache_kv,
    norm_gain,
    w_query,
    w_keyval,
    w_out,
):
    n = lax.axis_size("tensor")
    m = lax.axis_size("dp")
    requests, feat = root_features.shape
    own_requests = cache_lengths.shape[0]
    rows = requests * BRANCH
    own = own_requests * BRANCH
    share = feat // n
    head_cols = w_query.shape[1]
    proj_cols = head_cols + 2 * HD

    def one_hots(table):
        count = table.shape[0]
        first = (jnp.arange(count, dtype=jnp.int32) * BRANCH)[None, :, None]
        index = (jnp.swapaxes(table, 0, 1) + first).reshape(DEPTHS - 1, count * BRANCH)
        lane = jnp.arange(count * BRANCH, dtype=jnp.int32)
        return (index[:, :, None] == lane[None, None, :]).astype(jnp.bfloat16)

    hot = one_hots(parents)
    own_parents = lax.dynamic_slice_in_dim(
        parents, lax.axis_index("dp") * own_requests, own_requests, 0
    )
    own_hot = jnp.pad(one_hots(own_parents), ((1, 0), (0, 0), (0, 0)))
    bf16, f32 = jnp.bfloat16, jnp.float32
    vmem = pl.BlockSpec(memory_space=pltpu.VMEM)
    smem = pl.BlockSpec(memory_space=pltpu.SMEM)
    hbm = pl.BlockSpec(memory_space=pl.ANY)
    dma = pltpu.SemaphoreType.DMA
    return pl.pallas_call(
        functools.partial(tree_kernel, n, m),
        out_shape=jax.ShapeDtypeStruct((requests, DEPTHS, BRANCH, share), bf16),
        in_specs=[vmem, hbm, vmem, vmem, smem, hbm, vmem, hbm, hbm, hbm],
        out_specs=vmem,
        scratch_shapes=[
            pltpu.VMEM((requests, BRANCH, feat), bf16),
            pltpu.VMEM((DEPTHS - 1, requests, BRANCH, share), bf16),
            pltpu.VMEM(cache_kv.shape, bf16),
            pltpu.VMEM((feat, head_cols), bf16),
            pltpu.VMEM((feat, 2 * HD), bf16),
            pltpu.VMEM((head_cols, feat), bf16),
            pltpu.VMEM((DEPTHS, n, rows, share), bf16),
            pltpu.VMEM((DEPTHS, n, 8, rows), f32),
            pltpu.VMEM((rows, share), f32),
            pltpu.VMEM((rows, proj_cols), f32),
            pltpu.VMEM((DEPTHS, m, own, proj_cols), bf16),
            pltpu.VMEM((DEPTHS, m - 1, own, proj_cols), bf16),
            pltpu.VMEM((DEPTHS, 8, rows), f32),
            pltpu.VMEM((DEPTHS, m - 1, 8, rows), f32),
            pltpu.VMEM((DEPTHS * own, HD), bf16),
            pltpu.VMEM((DEPTHS * own, HD), bf16),
            pltpu.VMEM((own, DEPTHS * own), bf16),
            pltpu.VMEM((DEPTHS, m, own, head_cols), bf16),
            pltpu.VMEM((n, rows, share), f32),
            pltpu.VMEM((DEPTHS, n, rows, share), bf16),
            pltpu.VMEM((DEPTHS, n + 1, rows, share), bf16),
            pltpu.VMEM((rows, share), f32),
            dma((4 + DEPTHS,)),
            dma((DEPTHS, n + 1)),
            dma((DEPTHS, n)),
            dma((DEPTHS, n - 1)),
            dma((DEPTHS, n - 1)),
            dma((DEPTHS, m - 1)),
            dma((DEPTHS, m - 1)),
            dma((DEPTHS, m - 1)),
            dma((DEPTHS, m - 1)),
            dma((DEPTHS, m - 1)),
            dma((DEPTHS, m - 1)),
            dma((DEPTHS, n)),
            dma((DEPTHS, n + 1)),
        ],
        compiler_params=pltpu.CompilerParams(
            collective_id=0, has_side_effects=True, vmem_limit_bytes=60 * 1024 * 1024
        ),
    )(
        root_features,
        branch_embeds,
        hot,
        own_hot,
        cache_lengths,
        cache_kv,
        norm_gain.astype(f32)[None, :],
        w_query,
        w_keyval.reshape(feat, 2 * HD),
        w_out,
    )


def solution(mesh):
    in_line = 1 < mesh.shape["tensor"] <= 8 and mesh.shape["dp"] > 1
    return jax.shard_map(
        kernel_shards if in_line else shards,
        mesh=mesh,
        in_specs=(
            P("groups", "dp"),
            P("groups", None, None, "dp"),
            P("groups", None, None),
            P(("groups", "dp")),
            P(("groups", "dp"), None, None, "tensor"),
            P("dp"),
            P("dp", "tensor"),
            P("dp", None, "tensor"),
            P("tensor", "dp"),
        ),
        out_specs=P("groups", None, None, ("dp", "tensor")),
        check_vma=False,
    )
```

```python
import functools

import jax
import jax.numpy as jnp
from jax import lax
from jax.experimental import pallas as pl
from jax.experimental.pallas import tpu as pltpu
from jax.sharding import PartitionSpec as P

D = 16384
HD = 128
BRANCH = 8
DEPTHS = 4
CACHE = 512
BATCHES = 2


epsilon = 1e-05
masked_score = -1e30


def ancestor_path(parent_table, tree_level):
    current = jnp.broadcast_to(
        jnp.arange(BRANCH, dtype=jnp.int32)[None, :], (parent_table.shape[0], BRANCH)
    )
    path_nodes = [current]
    for upper in range(tree_level, 0, -1):
        current = jnp.take_along_axis(parent_table[:, upper - 1], current, axis=1)
        path_nodes.append(current)
    return path_nodes[::-1]


def tree_mask_of(parent_table, tree_level):
    path_nodes = ancestor_path(parent_table, tree_level)
    columns = jnp.arange(BRANCH, dtype=jnp.int32)
    blocks = []
    for other_level in range(DEPTHS):
        if other_level <= tree_level:
            blocks.append(columns[None, None, :] == path_nodes[other_level][:, :, None])
        else:
            blocks.append(jnp.zeros((parent_table.shape[0], BRANCH, BRANCH), dtype=bool))
    return jnp.concatenate(blocks, axis=2)


def shards(
    root_features,
    branch_embeds,
    parents,
    cache_lengths,
    cache_kv,
    norm_gain,
    w_query,
    w_keyval,
    w_out,
):
    request_count, feat_cols = root_features.shape
    local_requests = cache_lengths.shape[0]
    head_cols = w_query.shape[1]
    kv_cols = w_keyval.shape[2]
    kv_local = kv_cols // HD
    all_rows = request_count * BRANCH
    own_rows = local_requests * BRANCH
    share_cols = feat_cols // lax.axis_size("tensor")
    dp_index = lax.axis_index("dp")
    tensor_index = lax.axis_index("tensor")
    weights = jnp.concatenate([w_query, w_keyval.reshape(feat_cols, 2 * kv_cols)], axis=1)
    gain = norm_gain.astype(jnp.float32)
    own_parents = lax.dynamic_slice_in_dim(parents, dp_index * local_requests, local_requests, 0)
    cache_keys = cache_kv[:, 0].reshape(local_requests, CACHE, kv_local, HD)
    cache_values = cache_kv[:, 1].reshape(local_requests, CACHE, kv_local, HD)
    positions = jnp.arange(CACHE, dtype=jnp.int32)
    cache_valid = positions[None, :] < cache_lengths[:, None]
    tree_keys = jnp.zeros((local_requests, DEPTHS * BRANCH, kv_local, HD), jnp.bfloat16)
    tree_values = jnp.zeros((local_requests, DEPTHS * BRANCH, kv_local, HD), jnp.bfloat16)
    results = []
    previous = None
    for tree_level in range(DEPTHS):
        if tree_level == 0:
            parent = jnp.broadcast_to(root_features[:, None, :], (request_count, BRANCH, feat_cols))
        else:
            parent = jnp.take_along_axis(previous, parents[:, tree_level - 1][:, :, None], axis=1)
        node_state = parent.astype(jnp.float32) + branch_embeds[:, tree_level].astype(jnp.float32)
        flat_state = node_state.reshape(all_rows, feat_cols)
        square_sums = jnp.sum(flat_state * flat_state, axis=1)
        scaled = (flat_state * gain).astype(jnp.bfloat16)
        total_sums = lax.psum(square_sums, "dp")
        own_sums = lax.dynamic_slice_in_dim(total_sums, dp_index * own_rows, own_rows, 0)
        proj_terms = lax.psum_scatter(
            jnp.dot(scaled, weights, preferred_element_type=jnp.float32).astype(jnp.bfloat16),
            "dp",
            scatter_dimension=0,
            tiled=True,
        ).astype(jnp.float32)
        inv_rms = lax.rsqrt(own_sums / D + epsilon)[:, None]
        projected = (proj_terms * inv_rms).astype(jnp.bfloat16)
        queries = projected[:, :head_cols].reshape(local_requests, BRANCH, kv_local, -1, HD)
        new_keys = projected[:, head_cols : head_cols + kv_cols].reshape(
            local_requests, BRANCH, kv_local, HD
        )
        new_values = projected[:, head_cols + kv_cols :].reshape(
            local_requests, BRANCH, kv_local, HD
        )
        tree_keys = tree_keys.at[:, tree_level * BRANCH : (tree_level + 1) * BRANCH].set(new_keys)
        tree_values = tree_values.at[:, tree_level * BRANCH : (tree_level + 1) * BRANCH].set(
            new_values
        )
        tree_mask = tree_mask_of(own_parents, tree_level)
        cache_scores = jnp.einsum(
            "rbkgd,rckd->rkgbc", queries, cache_keys, preferred_element_type=jnp.float32
        ) * HD ** (-0.5)
        tree_scores = jnp.einsum(
            "rbkgd,rtkd->rkgbt", queries, tree_keys, preferred_element_type=jnp.float32
        ) * HD ** (-0.5)
        cache_scores = jnp.where(cache_valid[:, None, None, None, :], cache_scores, masked_score)
        tree_scores = jnp.where(tree_mask[:, None, None, :, :], tree_scores, masked_score)
        row_max = jnp.maximum(jnp.max(cache_scores, axis=4), jnp.max(tree_scores, axis=4))[
            ..., None
        ]
        cache_exp = jnp.exp(cache_scores - row_max)
        tree_exp = jnp.exp(tree_scores - row_max)
        denominator = jnp.sum(cache_exp, axis=4, keepdims=True) + jnp.sum(
            tree_exp, axis=4, keepdims=True
        )
        cache_weights = (cache_exp / denominator).astype(jnp.bfloat16)
        tree_weights = (tree_exp / denominator).astype(jnp.bfloat16)
        mixed = jnp.einsum(
            "rkgbc,rckd->rbkgd", cache_weights, cache_values, preferred_element_type=jnp.float32
        )
        mixed = mixed + jnp.einsum(
            "rkgbt,rtkd->rbkgd", tree_weights, tree_values, preferred_element_type=jnp.float32
        )
        attended = mixed.reshape(own_rows, head_cols).astype(jnp.bfloat16)
        partial_out = jnp.dot(
            lax.all_gather(attended, "dp", axis=0, tiled=True),
            w_out,
            preferred_element_type=jnp.float32,
        )
        share_sums = lax.psum_scatter(
            partial_out.astype(jnp.bfloat16), "tensor", scatter_dimension=1, tiled=True
        ).astype(jnp.float32)
        residual = lax.dynamic_slice_in_dim(flat_state, tensor_index * share_cols, share_cols, 1)
        fresh_share = (residual + share_sums).astype(jnp.bfloat16)
        if tree_level + 1 < DEPTHS:
            gathered = lax.all_gather(fresh_share, "tensor", axis=1, tiled=True)
            previous = gathered.reshape(request_count, BRANCH, feat_cols)
        results.append(fresh_share.reshape(request_count, BRANCH, share_cols))
    return jnp.stack(results, axis=1)


MESH = pl.DeviceIdType.MESH


def dot32(a, b):
    return jnp.dot(a, b, preferred_element_type=jnp.float32)


def dot32_t(a, b):
    return lax.dot_general(a, b, (((1,), (1,)), ((), ())), preferred_element_type=jnp.float32)


def tree_kernel(
    n,
    m,
    root_ref,
    emb_hbm,
    hot_ref,
    own_hot_ref,
    len_ref,
    cache_hbm,
    gain_ref,
    wq_hbm,
    wkv_hbm,
    wo_hbm,
    out_ref,
    emb0,
    emb_share,
    cache,
    wq,
    wkv,
    wo,
    scaled,
    share_sums,
    state,
    proj,
    proj_send,
    proj_recv,
    sums_send,
    sums_recv,
    tree_keys,
    tree_values,
    tree_mask,
    att,
    part,
    rs_send,
    rs_recv,
    total,
    load_sem,
    ag_ssem,
    ag_rsem,
    tsum_ssem,
    tsum_rsem,
    proj_ssem,
    proj_rsem,
    dsum_ssem,
    dsum_rsem,
    att_ssem,
    att_rsem,
    rs_ssem,
    rs_rsem,
):
    t = lax.axis_index("tensor")
    d = lax.axis_index("dp")
    requests, feat = root_ref.shape
    own_requests = requests // m
    part_requests = own_requests // BATCHES
    own = part_requests * BRANCH
    rows = own * m
    lanes = sums_send.shape[2]
    share = feat // n
    head_cols = wq.shape[1]
    heads = head_cols // HD
    steps = BATCHES * DEPTHS

    def cols_of(s):
        return pl.ds(pl.multiple_of(s * share, share), share)

    def batch_rows(b):
        return [pl.ds(k * own_requests + b * part_requests, part_requests) for k in range(m)]

    def joined(blocks, columns):
        return jnp.concatenate(blocks, axis=0).astype(jnp.float32).reshape(rows, columns)

    loads = [
        pltpu.make_async_copy(emb_hbm.at[:, 0], emb0, load_sem.at[0]),
        pltpu.make_async_copy(wq_hbm, wq, load_sem.at[1]),
        pltpu.make_async_copy(wkv_hbm, wkv, load_sem.at[2]),
        pltpu.make_async_copy(cache_hbm, cache, load_sem.at[3]),
        pltpu.make_async_copy(wo_hbm, wo, load_sem.at[4]),
    ]
    for e in range(1, DEPTHS):
        loads.append(
            pltpu.make_async_copy(
                emb_hbm.at[:, e, :, cols_of(t)], emb_share.at[e - 1], load_sem.at[4 + e]
            )
        )
    for load in loads:
        load.start()

    dp_to = [lax.rem(d + k, m) for k in range(1, m)]
    t_to = [lax.rem(t + k, n) for k in range(1, n)]

    barrier = pltpu.get_barrier_semaphore()
    for peer in dp_to:
        pl.semaphore_signal(barrier, inc=1, device_id={"dp": peer}, device_id_type=MESH)
    for peer in t_to:
        pl.semaphore_signal(barrier, inc=1, device_id={"tensor": peer}, device_id_type=MESH)
    pl.semaphore_wait(barrier, m + n - 2)

    def ag_copy(e, s, to, send_slot):
        return pltpu.make_async_remote_copy(
            src_ref=scaled.at[e, s],
            dst_ref=scaled.at[e, s],
            send_sem=ag_ssem.at[e, send_slot],
            recv_sem=ag_rsem.at[e, s],
            device_id={"tensor": to},
            device_id_type=MESH,
        )

    def tsum_copy(e, k):
        return pltpu.make_async_remote_copy(
            src_ref=share_sums.at[e, n - 1],
            dst_ref=share_sums.at[e, k],
            send_sem=tsum_ssem.at[e, k],
            recv_sem=tsum_rsem.at[e, k],
            device_id={"tensor": t_to[k]},
            device_id_type=MESH,
        )

    def proj_copy(e, k):
        return pltpu.make_async_remote_copy(
            src_ref=proj_send.at[e, dp_to[k]],
            dst_ref=proj_recv.at[e, k],
            send_sem=proj_ssem.at[e, k],
            recv_sem=proj_rsem.at[e, k],
            device_id={"dp": dp_to[k]},
            device_id_type=MESH,
        )

    def dsum_copy(e, k):
        return pltpu.make_async_remote_copy(
            src_ref=sums_send.at[e],
            dst_ref=sums_recv.at[e, k],
            send_sem=dsum_ssem.at[e, k],
            recv_sem=dsum_rsem.at[e, k],
            device_id={"dp": dp_to[k]},
            device_id_type=MESH,
        )

    def att_copy(e, k):
        return pltpu.make_async_remote_copy(
            src_ref=att.at[e, d],
            dst_ref=att.at[e, d],
            send_sem=att_ssem.at[e, k],
            recv_sem=att_rsem.at[e, k],
            device_id={"dp": dp_to[k]},
            device_id_type=MESH,
        )

    def rs_copy(e, s, to, slot):
        return pltpu.make_async_remote_copy(
            src_ref=rs_send.at[e, s],
            dst_ref=rs_recv.at[e, slot],
            send_sem=rs_ssem.at[e, s],
            recv_sem=rs_rsem.at[e, slot],
            device_id={"tensor": to},
            device_id_type=MESH,
        )

    def rs_right(e, s):
        return rs_copy(e, s, t + 1, s)

    def rs_left(e, s):
        return rs_copy(e, s, t - 1, jnp.where(t - 1 == s, n, s))

    def rs_wait(e, slot):
        rs_copy(e, 0, lax.rem(t + 1, n), slot).wait_recv()

    eye = lax.broadcasted_iota(jnp.int32, (rows, lanes), 0) == lax.broadcasted_iota(
        jnp.int32, (rows, lanes), 1
    )

    def to_lanes(column):
        spread = jnp.where(eye, jnp.broadcast_to(column, (rows, lanes)), 0.0)
        return jnp.broadcast_to(jnp.sum(spread, axis=0, keepdims=True), (8, lanes))

    def product(i, s, first=False):
        block = scaled[i, s]
        if first:
            proj[:, :head_cols] = dot32(block, wq[cols_of(s)])
            proj[:, head_cols:] = dot32(block, wkv[cols_of(s)])
        else:
            proj[:, :head_cols] += dot32(block, wq[cols_of(s)])
            proj[:, head_cols:] += dot32(block, wkv[cols_of(s)])

    def gather_wave(i, k):
        before = t - k
        after = t + k

        @pl.when(before >= 0)
        def _():
            ag_copy(i, before, lax.rem(t + 1, n), before).wait_recv()

            @pl.when(t < n - 1)
            def _():
                ag_copy(i, before, t + 1, before).start()

        @pl.when(after < n)
        def _():
            ag_copy(i, after, lax.rem(t + 1, n), after).wait_recv()

            @pl.when(t > 0)
            def _():
                ag_copy(i, after, t - 1, after).start()

        @pl.when(before >= 0)
        def _():
            product(i, before)

        @pl.when(after < n)
        def _():
            product(i, after)

    def add_arrived(i, s):
        rs_wait(i, s)
        rs_send[i, s] = (part[s] + rs_recv[i, s].astype(jnp.float32)).astype(jnp.bfloat16)

    def sum_wave(i, w):
        right = n - 1 + t - w
        left = w - (n - 1 - t)

        @pl.when((t > 0) & (right <= n - 1) & (right > t))
        def _():
            add_arrived(i, right)
            rs_right(i, right).start()

        @pl.when((t < n - 1) & (left >= 0) & (left < t))
        def _():
            add_arrived(i, left)
            rs_left(i, left).start()

    def finish(i):
        b = lax.rem(i, BATCHES)
        e = i // BATCHES
        total[...] = state[b] + part[t]

        @pl.when(t > 0)
        def _():
            rs_wait(i, t)
            total[...] += rs_recv[i, t].astype(jnp.float32)

        @pl.when(t < n - 1)
        def _():
            rs_wait(i, n)
            total[...] += rs_recv[i, n].astype(jnp.float32)

        fresh = total[...]

        @pl.when(e < DEPTHS - 1)
        def _():
            later = i + BATCHES
            embeds = joined([emb_share[e, r] for r in batch_rows(b)], share)
            node = dot32(hot_ref[i], fresh.astype(jnp.bfloat16)) + embeds
            state[b] = node
            scaled[later, t] = (node * gain_ref[:, cols_of(t)]).astype(jnp.bfloat16)

            @pl.when(t < n - 1)
            def _():
                ag_copy(later, t, t + 1, t).start()

            @pl.when(t > 0)
            def _():
                ag_copy(later, t, t - 1, n).start()

            share_sums[later, n - 1] = to_lanes(jnp.sum(node * node, axis=1, keepdims=True))
            for k in range(n - 1):
                tsum_copy(later, k).start()

        for k, r in enumerate(batch_rows(b)):
            out_ref[r, pl.ds(e, 1)] = (
                fresh[k * own : (k + 1) * own]
                .reshape(part_requests, 1, BRANCH, share)
                .astype(jnp.bfloat16)
            )

    row_id = lax.broadcasted_iota(jnp.int32, (rows, requests), 0)
    request_id = lax.broadcasted_iota(jnp.int32, (rows, requests), 1)
    loads[0].wait()

    def first_states(b, carry):
        place = row_id // BRANCH
        request = (
            place // part_requests * own_requests + b * part_requests + place % part_requests
        )
        root_hot = (request == request_id).astype(jnp.bfloat16)
        squares = jnp.zeros((rows, 1), jnp.float32)
        for s in range(n):
            cols = slice(s * share, (s + 1) * share)
            embeds = joined([emb0[r, :, cols] for r in batch_rows(b)], share)
            node = dot32(root_hot, root_ref[:, cols]) + embeds
            squares = squares + jnp.sum(node * node, axis=1, keepdims=True)
            scaled[b, s] = (node * gain_ref[:, cols]).astype(jnp.bfloat16)

            @pl.when(t == s)
            def _():
                state[b] = node

        sums_send[b] = to_lanes(squares)
        return carry

    lax.fori_loop(0, BATCHES, first_states, 0)
    tree_keys[...] = jnp.zeros_like(tree_keys)
    tree_values[...] = jnp.zeros_like(tree_values)
    tree_mask[...] = jnp.zeros_like(tree_mask)
    loads[1].wait()
    loads[2].wait()

    def step(i, carry):
        b = lax.rem(i, BATCHES)
        e = i // BATCHES
        later = i + BATCHES - 1
        gathering = (i > 0) & (later < steps)

        @pl.when(e == 0)
        def _():
            product(i, 0, True)
            for s in range(1, n):
                product(i, s)

        @pl.when(e > 0)
        def _():
            gather_wave(i, n - 1)
            summed = share_sums[i, n - 1]
            for k in range(n - 1):
                tsum_copy(i, k).wait_recv()
                summed = summed + share_sums[i, k]
            sums_send[i] = summed

        for k in range(m):
            proj_send[i, k] = proj[k * own : (k + 1) * own].astype(jnp.bfloat16)
        for k in range(m - 1):
            proj_copy(i, k).start()
            dsum_copy(i, k).start()

        @pl.when(i > 0)
        def _():
            for w in range(2, n - 1):
                sum_wave(i - 1, w)

        own_row = lax.broadcasted_iota(jnp.int32, (own, DEPTHS * own), 0)
        own_col = lax.broadcasted_iota(jnp.int32, (own, DEPTHS * own), 1)
        itself = (own_col == own_row + e * own).astype(jnp.float32)
        mask_now = itself + dot32(own_hot_ref[i], tree_mask[b])
        tree_mask[b] = mask_now.astype(jnp.bfloat16)

        projected = proj[pl.ds(pl.multiple_of(d * own, own), own)]
        summed = sums_send[i]
        for k in range(m - 1):
            proj_copy(i, k).wait_recv()
            dsum_copy(i, k).wait_recv()
            projected = projected + proj_recv[i, k].astype(jnp.float32)
            summed = summed + sums_recv[i, k]
        pick = lax.broadcasted_iota(jnp.int32, (own, lanes), 1) == (
            lax.broadcasted_iota(jnp.int32, (own, lanes), 0) + d * own
        )
        own_sums = jnp.sum(
            jnp.where(pick, jnp.broadcast_to(summed[0:1], (own, lanes)), 0.0),
            axis=1,
            keepdims=True,
        )
        inv_rms = lax.rsqrt(own_sums / (feat * m) + epsilon)
        projected = projected * inv_rms
        queries = jnp.concatenate(
            [
                projected[:, h * HD : (h + 1) * HD].reshape(part_requests, 1, BRANCH, HD)
                for h in range(heads)
            ],
            axis=1,
        ).reshape(own * heads, HD).astype(jnp.bfloat16)
        now = pl.ds(pl.multiple_of(e * own, own), own)
        tree_keys[b, now] = projected[:, head_cols : head_cols + HD].astype(jnp.bfloat16)
        tree_values[b, now] = projected[:, head_cols + HD :].astype(jnp.bfloat16)

        @pl.when(i == 0)
        def _():
            loads[3].wait()

        per = heads * BRANCH
        tree_scores = dot32_t(queries, tree_keys[b]) * HD ** (-0.5)
        allowed = jnp.broadcast_to(
            mask_now.reshape(part_requests, 1, BRANCH, DEPTHS * own),
            (part_requests, heads, BRANCH, DEPTHS * own),
        ).reshape(own * heads, DEPTHS * own)
        tree_scores = jnp.where(allowed > 0.5, tree_scores, masked_score)
        cache_scores = []
        position = lax.broadcasted_iota(jnp.int32, (per, CACHE), 1)
        for r in range(part_requests):
            request = b * part_requests + r
            scores = dot32_t(queries[r * per : (r + 1) * per], cache[request, 0]) * HD ** (-0.5)
            cache_scores.append(jnp.where(position < len_ref[request], scores, masked_score))
        cache_scores = jnp.concatenate(cache_scores, axis=0)
        row_max = jnp.maximum(
            jnp.max(cache_scores, axis=1, keepdims=True),
            jnp.max(tree_scores, axis=1, keepdims=True),
        )
        cache_exp = jnp.exp(cache_scores - row_max)
        tree_exp = jnp.exp(tree_scores - row_max)
        denominator = jnp.sum(cache_exp, axis=1, keepdims=True) + jnp.sum(
            tree_exp, axis=1, keepdims=True
        )
        cache_weights = (cache_exp / denominator).astype(jnp.bfloat16)
        tree_weights = (tree_exp / denominator).astype(jnp.bfloat16)
        mixed = jnp.concatenate(
            [
                dot32(cache_weights[r * per : (r + 1) * per], cache[b * part_requests + r, 1])
                for r in range(part_requests)
            ],
            axis=0,
        ) + dot32(tree_weights, tree_values[b])
        mixed = mixed.reshape(part_requests, heads, BRANCH, HD)
        for h in range(heads):
            att[i, d, :, h * HD : (h + 1) * HD] = mixed[:, h].reshape(own, HD).astype(jnp.bfloat16)
        for k in range(m - 1):
            att_copy(i, k).start()

        @pl.when(i > 0)
        def _():
            finish(i - 1)

        @pl.when(gathering)
        def _():
            product(later, t, True)

        for k in range(m - 1):
            att_copy(i, k).wait_recv()

        @pl.when(i == 0)
        def _():
            for load in loads[4:]:
                load.wait()

        attended = att[i].reshape(rows, head_cols)
        done = set()
        for k in range(n):
            right, left = n - 1 - k, k
            for s in (right, left):
                if s not in done:
                    part[s] = dot32(attended, wo[:, s * share : (s + 1) * share])
                    done.add(s)
            if k < n - 1:

                @pl.when(t == 0)
                def _():
                    rs_send[i, right] = part[right].astype(jnp.bfloat16)
                    rs_right(i, right).start()

                @pl.when(t == n - 1)
                def _():
                    rs_send[i, left] = part[left].astype(jnp.bfloat16)
                    rs_left(i, left).start()

        if n > 2:

            @pl.when(gathering)
            def _():
                gather_wave(later, 1)

            sum_wave(i, 1)

            @pl.when(gathering)
            def _():
                for k in range(2, n - 1):
                    gather_wave(later, k)

        return carry

    lax.fori_loop(0, steps, step, 0)
    for w in range(2, n - 1):
        sum_wave(steps - 1, w)
    finish(steps - 1)

    def drain(i, carry):
        for k in range(m - 1):
            proj_copy(i, k).wait_send()
            dsum_copy(i, k).wait_send()
            att_copy(i, k).wait_send()
        for s in range(n):

            @pl.when(t < s)
            def _():
                rs_right(i, s).wait_send()

            @pl.when(t > s)
            def _():
                rs_left(i, s).wait_send()

        @pl.when(i >= BATCHES)
        def _():
            for k in range(n - 1):
                tsum_copy(i, k).wait_send()
            for s in range(n):

                @pl.when((s <= t) & (t < n - 1))
                def _():
                    ag_copy(i, s, t + 1, s).wait_send()

                @pl.when((s > t) & (t > 0))
                def _():
                    ag_copy(i, s, t - 1, s).wait_send()

            @pl.when(t > 0)
            def _():
                ag_copy(i, t, t - 1, n).wait_send()

        return carry

    lax.fori_loop(0, steps, drain, 0)


def kernel_shards(
    root_features,
    branch_embeds,
    parents,
    cache_lengths,
    cache_kv,
    norm_gain,
    w_query,
    w_keyval,
    w_out,
):
    n = lax.axis_size("tensor")
    m = lax.axis_size("dp")
    requests, feat = root_features.shape
    own_requests = cache_lengths.shape[0]
    part_requests = own_requests // BATCHES
    own = part_requests * BRANCH
    rows = own * m
    lanes = -(-rows // 128) * 128
    steps = BATCHES * DEPTHS
    share = feat // n
    head_cols = w_query.shape[1]
    proj_cols = head_cols + 2 * HD

    def one_hots(table):
        devices = table.shape[0] // own_requests
        count = devices * own
        split = table.reshape(devices, BATCHES, part_requests, DEPTHS - 1, BRANCH)
        split = jnp.transpose(split, (3, 1, 0, 2, 4)).reshape((DEPTHS - 1) * BATCHES, count)
        lane = jnp.arange(count, dtype=jnp.int32)
        index = split + (lane // BRANCH * BRANCH)[None, :]
        return (index[:, :, None] == lane[None, None, :]).astype(jnp.bfloat16)

    hot = one_hots(parents)
    own_parents = lax.dynamic_slice_in_dim(
        parents, lax.axis_index("dp") * own_requests, own_requests, 0
    )
    own_hot = jnp.pad(one_hots(own_parents), ((BATCHES, 0), (0, 0), (0, 0)))
    bf16, f32 = jnp.bfloat16, jnp.float32
    vmem = pl.BlockSpec(memory_space=pltpu.VMEM)
    smem = pl.BlockSpec(memory_space=pltpu.SMEM)
    hbm = pl.BlockSpec(memory_space=pl.ANY)
    dma = pltpu.SemaphoreType.DMA
    return pl.pallas_call(
        functools.partial(tree_kernel, n, m),
        out_shape=jax.ShapeDtypeStruct((requests, DEPTHS, BRANCH, share), bf16),
        in_specs=[vmem, hbm, vmem, vmem, smem, hbm, vmem, hbm, hbm, hbm],
        out_specs=vmem,
        scratch_shapes=[
            pltpu.VMEM((requests, BRANCH, feat), bf16),
            pltpu.VMEM((DEPTHS - 1, requests, BRANCH, share), bf16),
            pltpu.VMEM(cache_kv.shape, bf16),
            pltpu.VMEM((feat, head_cols), bf16),
            pltpu.VMEM((feat, 2 * HD), bf16),
            pltpu.VMEM((head_cols, feat), bf16),
            pltpu.VMEM((steps, n, rows, share), bf16),
            pltpu.VMEM((steps, n, 8, lanes), f32),
            pltpu.VMEM((BATCHES, rows, share), f32),
            pltpu.VMEM((rows, proj_cols), f32),
            pltpu.VMEM((steps, m, own, proj_cols), bf16),
            pltpu.VMEM((steps, m - 1, own, proj_cols), bf16),
            pltpu.VMEM((steps, 8, lanes), f32),
            pltpu.VMEM((steps, m - 1, 8, lanes), f32),
            pltpu.VMEM((BATCHES, DEPTHS * own, HD), bf16),
            pltpu.VMEM((BATCHES, DEPTHS * own, HD), bf16),
            pltpu.VMEM((BATCHES, own, DEPTHS * own), bf16),
            pltpu.VMEM((steps, m, own, head_cols), bf16),
            pltpu.VMEM((n, rows, share), f32),
            pltpu.VMEM((steps, n, rows, share), bf16),
            pltpu.VMEM((steps, n + 1, rows, share), bf16),
            pltpu.VMEM((rows, share), f32),
            dma((4 + DEPTHS,)),
            dma((steps, n + 1)),
            dma((steps, n)),
            dma((steps, n - 1)),
            dma((steps, n - 1)),
            dma((steps, m - 1)),
            dma((steps, m - 1)),
            dma((steps, m - 1)),
            dma((steps, m - 1)),
            dma((steps, m - 1)),
            dma((steps, m - 1)),
            dma((steps, n)),
            dma((steps, n + 1)),
        ],
        compiler_params=pltpu.CompilerParams(
            collective_id=0, has_side_effects=True, vmem_limit_bytes=60 * 1024 * 1024
        ),
    )(
        root_features,
        branch_embeds,
        hot,
        own_hot,
        cache_lengths,
        cache_kv,
        norm_gain.astype(f32)[None, :],
        w_query,
        w_keyval.reshape(feat, 2 * HD),
        w_out,
    )


def solution(mesh):
    in_line = 1 < mesh.shape["tensor"] <= 8 and mesh.shape["dp"] > 1
    return jax.shard_map(
        kernel_shards if in_line else shards,
        mesh=mesh,
        in_specs=(
            P("groups", "dp"),
            P("groups", None, None, "dp"),
            P("groups", None, None),
            P(("groups", "dp")),
            P(("groups", "dp"), None, None, "tensor"),
            P("dp"),
            P("dp", "tensor"),
            P("dp", None, "tensor"),
            P("tensor", "dp"),
        ),
        out_specs=P("groups", None, None, ("dp", "tensor")),
        check_vma=False,
    )
```

```python
import functools

import jax
import jax.numpy as jnp
from jax import lax
from jax.experimental import pallas as pl
from jax.experimental.pallas import tpu as pltpu
from jax.sharding import PartitionSpec as P

D = 16384
HD = 128
BRANCH = 8
DEPTHS = 4
CACHE = 512
BATCHES = 2
SUBS = 2


epsilon = 1e-05
masked_score = -1e30


def ancestor_path(parent_table, tree_level):
    current = jnp.broadcast_to(
        jnp.arange(BRANCH, dtype=jnp.int32)[None, :], (parent_table.shape[0], BRANCH)
    )
    path_nodes = [current]
    for upper in range(tree_level, 0, -1):
        current = jnp.take_along_axis(parent_table[:, upper - 1], current, axis=1)
        path_nodes.append(current)
    return path_nodes[::-1]


def tree_mask_of(parent_table, tree_level):
    path_nodes = ancestor_path(parent_table, tree_level)
    columns = jnp.arange(BRANCH, dtype=jnp.int32)
    blocks = []
    for other_level in range(DEPTHS):
        if other_level <= tree_level:
            blocks.append(columns[None, None, :] == path_nodes[other_level][:, :, None])
        else:
            blocks.append(jnp.zeros((parent_table.shape[0], BRANCH, BRANCH), dtype=bool))
    return jnp.concatenate(blocks, axis=2)


def shards(
    root_features,
    branch_embeds,
    parents,
    cache_lengths,
    cache_kv,
    norm_gain,
    w_query,
    w_keyval,
    w_out,
):
    request_count, feat_cols = root_features.shape
    local_requests = cache_lengths.shape[0]
    head_cols = w_query.shape[1]
    kv_cols = w_keyval.shape[2]
    kv_local = kv_cols // HD
    all_rows = request_count * BRANCH
    own_rows = local_requests * BRANCH
    share_cols = feat_cols // lax.axis_size("tensor")
    dp_index = lax.axis_index("dp")
    tensor_index = lax.axis_index("tensor")
    weights = jnp.concatenate([w_query, w_keyval.reshape(feat_cols, 2 * kv_cols)], axis=1)
    gain = norm_gain.astype(jnp.float32)
    own_parents = lax.dynamic_slice_in_dim(parents, dp_index * local_requests, local_requests, 0)
    cache_keys = cache_kv[:, 0].reshape(local_requests, CACHE, kv_local, HD)
    cache_values = cache_kv[:, 1].reshape(local_requests, CACHE, kv_local, HD)
    positions = jnp.arange(CACHE, dtype=jnp.int32)
    cache_valid = positions[None, :] < cache_lengths[:, None]
    tree_keys = jnp.zeros((local_requests, DEPTHS * BRANCH, kv_local, HD), jnp.bfloat16)
    tree_values = jnp.zeros((local_requests, DEPTHS * BRANCH, kv_local, HD), jnp.bfloat16)
    results = []
    previous = None
    for tree_level in range(DEPTHS):
        if tree_level == 0:
            parent = jnp.broadcast_to(root_features[:, None, :], (request_count, BRANCH, feat_cols))
        else:
            parent = jnp.take_along_axis(previous, parents[:, tree_level - 1][:, :, None], axis=1)
        node_state = parent.astype(jnp.float32) + branch_embeds[:, tree_level].astype(jnp.float32)
        flat_state = node_state.reshape(all_rows, feat_cols)
        square_sums = jnp.sum(flat_state * flat_state, axis=1)
        scaled = (flat_state * gain).astype(jnp.bfloat16)
        total_sums = lax.psum(square_sums, "dp")
        own_sums = lax.dynamic_slice_in_dim(total_sums, dp_index * own_rows, own_rows, 0)
        proj_terms = lax.psum_scatter(
            jnp.dot(scaled, weights, preferred_element_type=jnp.float32).astype(jnp.bfloat16),
            "dp",
            scatter_dimension=0,
            tiled=True,
        ).astype(jnp.float32)
        inv_rms = lax.rsqrt(own_sums / D + epsilon)[:, None]
        projected = (proj_terms * inv_rms).astype(jnp.bfloat16)
        queries = projected[:, :head_cols].reshape(local_requests, BRANCH, kv_local, -1, HD)
        new_keys = projected[:, head_cols : head_cols + kv_cols].reshape(
            local_requests, BRANCH, kv_local, HD
        )
        new_values = projected[:, head_cols + kv_cols :].reshape(
            local_requests, BRANCH, kv_local, HD
        )
        tree_keys = tree_keys.at[:, tree_level * BRANCH : (tree_level + 1) * BRANCH].set(new_keys)
        tree_values = tree_values.at[:, tree_level * BRANCH : (tree_level + 1) * BRANCH].set(
            new_values
        )
        tree_mask = tree_mask_of(own_parents, tree_level)
        cache_scores = jnp.einsum(
            "rbkgd,rckd->rkgbc", queries, cache_keys, preferred_element_type=jnp.float32
        ) * HD ** (-0.5)
        tree_scores = jnp.einsum(
            "rbkgd,rtkd->rkgbt", queries, tree_keys, preferred_element_type=jnp.float32
        ) * HD ** (-0.5)
        cache_scores = jnp.where(cache_valid[:, None, None, None, :], cache_scores, masked_score)
        tree_scores = jnp.where(tree_mask[:, None, None, :, :], tree_scores, masked_score)
        row_max = jnp.maximum(jnp.max(cache_scores, axis=4), jnp.max(tree_scores, axis=4))[
            ..., None
        ]
        cache_exp = jnp.exp(cache_scores - row_max)
        tree_exp = jnp.exp(tree_scores - row_max)
        denominator = jnp.sum(cache_exp, axis=4, keepdims=True) + jnp.sum(
            tree_exp, axis=4, keepdims=True
        )
        cache_weights = (cache_exp / denominator).astype(jnp.bfloat16)
        tree_weights = (tree_exp / denominator).astype(jnp.bfloat16)
        mixed = jnp.einsum(
            "rkgbc,rckd->rbkgd", cache_weights, cache_values, preferred_element_type=jnp.float32
        )
        mixed = mixed + jnp.einsum(
            "rkgbt,rtkd->rbkgd", tree_weights, tree_values, preferred_element_type=jnp.float32
        )
        attended = mixed.reshape(own_rows, head_cols).astype(jnp.bfloat16)
        partial_out = jnp.dot(
            lax.all_gather(attended, "dp", axis=0, tiled=True),
            w_out,
            preferred_element_type=jnp.float32,
        )
        share_sums = lax.psum_scatter(
            partial_out.astype(jnp.bfloat16), "tensor", scatter_dimension=1, tiled=True
        ).astype(jnp.float32)
        residual = lax.dynamic_slice_in_dim(flat_state, tensor_index * share_cols, share_cols, 1)
        fresh_share = (residual + share_sums).astype(jnp.bfloat16)
        if tree_level + 1 < DEPTHS:
            gathered = lax.all_gather(fresh_share, "tensor", axis=1, tiled=True)
            previous = gathered.reshape(request_count, BRANCH, feat_cols)
        results.append(fresh_share.reshape(request_count, BRANCH, share_cols))
    return jnp.stack(results, axis=1)


MESH = pl.DeviceIdType.MESH


def dot32(a, b):
    return jnp.dot(a, b, preferred_element_type=jnp.float32)


def dot32_t(a, b):
    return lax.dot_general(a, b, (((1,), (1,)), ((), ())), preferred_element_type=jnp.float32)


def tree_kernel(
    n,
    m,
    root_ref,
    emb_hbm,
    hot_ref,
    len_ref,
    cache_hbm,
    gain_ref,
    wq_hbm,
    wkv_hbm,
    wo_hbm,
    out_ref,
    emb0,
    emb_share,
    cache,
    wq,
    wkv,
    wo,
    scaled,
    share_sums,
    state,
    proj,
    proj_send,
    proj_recv,
    sums_send,
    sums_recv,
    tree_keys,
    tree_values,
    tree_mask,
    att,
    part,
    rs_send,
    rs_recv,
    total,
    load_sem,
    ag_ssem,
    ag_rsem,
    tsum_ssem,
    tsum_rsem,
    proj_ssem,
    proj_rsem,
    dsum_ssem,
    dsum_rsem,
    att_ssem,
    att_rsem,
    rs_ssem,
    rs_rsem,
):
    t = lax.axis_index("tensor")
    d = lax.axis_index("dp")
    requests, feat = root_ref.shape
    own_requests = requests // m
    part_requests = own_requests // BATCHES
    own = part_requests * BRANCH
    rows = own * m
    lanes = sums_send.shape[2]
    share = feat // n
    head_cols = wq.shape[1]
    heads = head_cols // HD
    steps = BATCHES * DEPTHS

    sub = share // SUBS

    def sub_of(s, u):
        return pl.ds(pl.multiple_of(s * share + u * sub, sub), sub)

    def cols_of(s):
        return pl.ds(pl.multiple_of(s * share, share), share)

    def batch_rows(b):
        return [pl.ds(k * own_requests + b * part_requests, part_requests) for k in range(m)]

    def joined(blocks, columns):
        return jnp.concatenate(blocks, axis=0).astype(jnp.float32).reshape(rows, columns)

    loads = [
        pltpu.make_async_copy(emb_hbm.at[:, 0], emb0, load_sem.at[0]),
        pltpu.make_async_copy(wq_hbm, wq, load_sem.at[1]),
        pltpu.make_async_copy(wkv_hbm, wkv, load_sem.at[2]),
        pltpu.make_async_copy(cache_hbm, cache, load_sem.at[3]),
        pltpu.make_async_copy(wo_hbm, wo, load_sem.at[4]),
    ]
    for e in range(1, DEPTHS):
        loads.append(
            pltpu.make_async_copy(
                emb_hbm.at[:, e, :, cols_of(t)], emb_share.at[e - 1], load_sem.at[4 + e]
            )
        )
    for load in loads:
        load.start()

    dp_to = [lax.rem(d + k, m) for k in range(1, m)]
    t_to = [lax.rem(t + k, n) for k in range(1, n)]

    barrier = pltpu.get_barrier_semaphore()
    for peer in dp_to:
        pl.semaphore_signal(barrier, inc=1, device_id={"dp": peer}, device_id_type=MESH)
    for peer in t_to:
        pl.semaphore_signal(barrier, inc=1, device_id={"tensor": peer}, device_id_type=MESH)
    pl.semaphore_wait(barrier, m + n - 2)

    def ag_copy(e, s, u, to, send_slot):
        return pltpu.make_async_remote_copy(
            src_ref=scaled.at[e, s, u],
            dst_ref=scaled.at[e, s, u],
            send_sem=ag_ssem.at[e, send_slot, u],
            recv_sem=ag_rsem.at[e, s, u],
            device_id={"tensor": to},
            device_id_type=MESH,
        )

    def tsum_copy(e, k):
        return pltpu.make_async_remote_copy(
            src_ref=share_sums.at[e, n - 1],
            dst_ref=share_sums.at[e, k],
            send_sem=tsum_ssem.at[e, k],
            recv_sem=tsum_rsem.at[e, k],
            device_id={"tensor": t_to[k]},
            device_id_type=MESH,
        )

    def proj_copy(e, k):
        return pltpu.make_async_remote_copy(
            src_ref=proj_send.at[e, dp_to[k]],
            dst_ref=proj_recv.at[e, k],
            send_sem=proj_ssem.at[e, k],
            recv_sem=proj_rsem.at[e, k],
            device_id={"dp": dp_to[k]},
            device_id_type=MESH,
        )

    def dsum_copy(e, k):
        return pltpu.make_async_remote_copy(
            src_ref=sums_send.at[e],
            dst_ref=sums_recv.at[e, k],
            send_sem=dsum_ssem.at[e, k],
            recv_sem=dsum_rsem.at[e, k],
            device_id={"dp": dp_to[k]},
            device_id_type=MESH,
        )

    def att_copy(e, k):
        return pltpu.make_async_remote_copy(
            src_ref=att.at[e, d],
            dst_ref=att.at[e, d],
            send_sem=att_ssem.at[e, k],
            recv_sem=att_rsem.at[e, k],
            device_id={"dp": dp_to[k]},
            device_id_type=MESH,
        )

    def rs_copy(e, s, u, to, slot):
        return pltpu.make_async_remote_copy(
            src_ref=rs_send.at[e, s, u],
            dst_ref=rs_recv.at[e, slot, u],
            send_sem=rs_ssem.at[e, s, u],
            recv_sem=rs_rsem.at[e, slot, u],
            device_id={"tensor": to},
            device_id_type=MESH,
        )

    def rs_right(e, s, u):
        return rs_copy(e, s, u, t + 1, s)

    def rs_left(e, s, u):
        return rs_copy(e, s, u, t - 1, jnp.where(t - 1 == s, n, s))

    def rs_wait(e, slot, u):
        rs_copy(e, 0, u, lax.rem(t + 1, n), slot).wait_recv()

    eye = lax.broadcasted_iota(jnp.int32, (rows, lanes), 0) == lax.broadcasted_iota(
        jnp.int32, (rows, lanes), 1
    )

    def to_lanes(column):
        spread = jnp.where(eye, jnp.broadcast_to(column, (rows, lanes)), 0.0)
        return jnp.broadcast_to(jnp.sum(spread, axis=0, keepdims=True), (8, lanes))

    def product(i, s, first=False):
        for u in range(SUBS):
            block = scaled[i, s, u]
            cols = sub_of(s, u)
            if first and u == 0:
                proj[:, :head_cols] = dot32(block, wq[cols])
                proj[:, head_cols:] = dot32(block, wkv[cols])
            else:
                proj[:, :head_cols] += dot32(block, wq[cols])
                proj[:, head_cols:] += dot32(block, wkv[cols])

    def gather_wave(i, k):
        before = t - k
        after = t + k

        for u in range(SUBS):

            @pl.when(before >= 0)
            def _():
                ag_copy(i, before, u, lax.rem(t + 1, n), before).wait_recv()

                @pl.when(t < n - 1)
                def _():
                    ag_copy(i, before, u, t + 1, before).start()

            @pl.when(after < n)
            def _():
                ag_copy(i, after, u, lax.rem(t + 1, n), after).wait_recv()

                @pl.when(t > 0)
                def _():
                    ag_copy(i, after, u, t - 1, after).start()

        @pl.when(before >= 0)
        def _():
            product(i, before)

        @pl.when(after < n)
        def _():
            product(i, after)

    def add_arrived(i, s, u):
        rs_wait(i, s, u)
        rs_send[i, s, u] = (part[s, u] + rs_recv[i, s, u].astype(jnp.float32)).astype(
            jnp.bfloat16
        )

    def sum_wave(i, w, u):
        right = n - 1 + t - w
        left = w - (n - 1 - t)

        @pl.when((t > 0) & (right <= n - 1) & (right > t))
        def _():
            add_arrived(i, right, u)
            rs_right(i, right, u).start()

        @pl.when((t < n - 1) & (left >= 0) & (left < t))
        def _():
            add_arrived(i, left, u)
            rs_left(i, left, u).start()

    def later_waves(i):
        for u in range(SUBS):
            for w in range(1 if u else 2, n - 1):
                sum_wave(i, w, u)

    def finish(i):
        b = lax.rem(i, BATCHES)
        e = i // BATCHES
        later = i + BATCHES
        more = e < DEPTHS - 1
        for u in range(SUBS):
            cols = slice(u * sub, (u + 1) * sub)
            total[u] = state[b, u] + part[t, u]

            @pl.when(t > 0)
            def _():
                rs_wait(i, t, u)
                total[u] += rs_recv[i, t, u].astype(jnp.float32)

            @pl.when(t < n - 1)
            def _():
                rs_wait(i, n, u)
                total[u] += rs_recv[i, n, u].astype(jnp.float32)

            @pl.when(more)
            def _():
                embeds = joined([emb_share[e, r, :, cols] for r in batch_rows(b)], sub)
                node = dot32(hot_ref[i], total[u].astype(jnp.bfloat16)) + embeds
                state[b, u] = node
                scaled[later, t, u] = (node * gain_ref[:, sub_of(t, u)].astype(jnp.float32)).astype(jnp.bfloat16)

                @pl.when(t < n - 1)
                def _():
                    ag_copy(later, t, u, t + 1, t).start()

                @pl.when(t > 0)
                def _():
                    ag_copy(later, t, u, t - 1, n).start()

        @pl.when(more)
        def _():
            squares = jnp.zeros((rows, 1), jnp.float32)
            for u in range(SUBS):
                node = state[b, u]
                squares = squares + jnp.sum(node * node, axis=1, keepdims=True)
            share_sums[later, n - 1] = to_lanes(squares)
            for k in range(n - 1):
                tsum_copy(later, k).start()

        for u in range(SUBS):
            for k, r in enumerate(batch_rows(b)):
                out_ref[r, pl.ds(e, 1), :, u * sub : (u + 1) * sub] = (
                    total[u, k * own : (k + 1) * own]
                    .reshape(part_requests, 1, BRANCH, sub)
                    .astype(jnp.bfloat16)
                )

    row_id = lax.broadcasted_iota(jnp.int32, (rows, requests), 0)
    request_id = lax.broadcasted_iota(jnp.int32, (rows, requests), 1)
    loads[0].wait()

    def first_states(b, carry):
        place = row_id // BRANCH
        request = (
            place // part_requests * own_requests + b * part_requests + place % part_requests
        )
        root_hot = (request == request_id).astype(jnp.bfloat16)
        squares = jnp.zeros((rows, 1), jnp.float32)
        for s in range(n):
            cols = slice(s * share, (s + 1) * share)
            embeds = joined([emb0[r, :, cols] for r in batch_rows(b)], share)
            node = dot32(root_hot, root_ref[:, cols]) + embeds
            squares = squares + jnp.sum(node * node, axis=1, keepdims=True)
            fed = (node * gain_ref[:, cols].astype(jnp.float32)).astype(jnp.bfloat16)
            for u in range(SUBS):
                scaled[b, s, u] = fed[:, u * sub : (u + 1) * sub]

            @pl.when(t == s)
            def _():
                for u in range(SUBS):
                    state[b, u] = node[:, u * sub : (u + 1) * sub]

        sums_send[b] = to_lanes(squares)
        return carry

    lax.fori_loop(0, BATCHES, first_states, 0)
    tree_keys[...] = jnp.zeros_like(tree_keys)
    tree_values[...] = jnp.zeros_like(tree_values)
    tree_mask[...] = jnp.zeros_like(tree_mask)
    loads[1].wait()
    loads[2].wait()

    def step(i, carry):
        b = lax.rem(i, BATCHES)
        e = i // BATCHES
        later = i + BATCHES - 1
        gathering = (i > 0) & (later < steps)

        @pl.when(e == 0)
        def _():
            product(i, 0, True)
            for s in range(1, n):
                product(i, s)

        @pl.when(e > 0)
        def _():
            gather_wave(i, n - 1)
            summed = share_sums[i, n - 1]
            for k in range(n - 1):
                tsum_copy(i, k).wait_recv()
                summed = summed + share_sums[i, k]
            sums_send[i] = summed

        for k in range(m):
            proj_send[i, k] = proj[k * own : (k + 1) * own].astype(jnp.bfloat16)
        for k in range(m - 1):
            proj_copy(i, k).start()
            dsum_copy(i, k).start()

        @pl.when(i > 0)
        def _():
            later_waves(i - 1)

        own_row = lax.broadcasted_iota(jnp.int32, (own, DEPTHS * own), 0)
        own_col = lax.broadcasted_iota(jnp.int32, (own, DEPTHS * own), 1)
        itself = (own_col == own_row + e * own).astype(jnp.float32)
        own_rows = pl.ds(pl.multiple_of(d * own, own), own)
        mask_now = itself + dot32(hot_ref[jnp.maximum(i - BATCHES, 0), own_rows], tree_mask[b])
        tree_mask[b, own_rows] = mask_now.astype(jnp.bfloat16)

        projected = proj[pl.ds(pl.multiple_of(d * own, own), own)]
        summed = sums_send[i]
        for k in range(m - 1):
            proj_copy(i, k).wait_recv()
            dsum_copy(i, k).wait_recv()
            projected = projected + proj_recv[i, k].astype(jnp.float32)
            summed = summed + sums_recv[i, k]
        pick = lax.broadcasted_iota(jnp.int32, (own, lanes), 1) == (
            lax.broadcasted_iota(jnp.int32, (own, lanes), 0) + d * own
        )
        own_sums = jnp.sum(
            jnp.where(pick, jnp.broadcast_to(summed[0:1], (own, lanes)), 0.0),
            axis=1,
            keepdims=True,
        )
        inv_rms = lax.rsqrt(own_sums / (feat * m) + epsilon)
        projected = projected * inv_rms
        queries = jnp.concatenate(
            [
                projected[:, h * HD : (h + 1) * HD].reshape(part_requests, 1, BRANCH, HD)
                for h in range(heads)
            ],
            axis=1,
        ).reshape(own * heads, HD).astype(jnp.bfloat16)
        now = pl.ds(pl.multiple_of(e * own, own), own)
        tree_keys[b, now] = projected[:, head_cols : head_cols + HD].astype(jnp.bfloat16)
        tree_values[b, now] = projected[:, head_cols + HD :].astype(jnp.bfloat16)

        @pl.when(i == 0)
        def _():
            loads[3].wait()

        per = heads * BRANCH
        tree_scores = dot32_t(queries, tree_keys[b]) * HD ** (-0.5)
        allowed = jnp.broadcast_to(
            mask_now.reshape(part_requests, 1, BRANCH, DEPTHS * own),
            (part_requests, heads, BRANCH, DEPTHS * own),
        ).reshape(own * heads, DEPTHS * own)
        tree_scores = jnp.where(allowed > 0.5, tree_scores, masked_score)
        cache_scores = []
        position = lax.broadcasted_iota(jnp.int32, (per, CACHE), 1)
        for r in range(part_requests):
            request = b * part_requests + r
            scores = dot32_t(queries[r * per : (r + 1) * per], cache[request, 0]) * HD ** (-0.5)
            cache_scores.append(jnp.where(position < len_ref[request], scores, masked_score))
        cache_scores = jnp.concatenate(cache_scores, axis=0)
        row_max = jnp.maximum(
            jnp.max(cache_scores, axis=1, keepdims=True),
            jnp.max(tree_scores, axis=1, keepdims=True),
        )
        cache_exp = jnp.exp(cache_scores - row_max)
        tree_exp = jnp.exp(tree_scores - row_max)
        denominator = jnp.sum(cache_exp, axis=1, keepdims=True) + jnp.sum(
            tree_exp, axis=1, keepdims=True
        )
        cache_weights = (cache_exp / denominator).astype(jnp.bfloat16)
        tree_weights = (tree_exp / denominator).astype(jnp.bfloat16)
        mixed = jnp.concatenate(
            [
                dot32(cache_weights[r * per : (r + 1) * per], cache[b * part_requests + r, 1])
                for r in range(part_requests)
            ],
            axis=0,
        ) + dot32(tree_weights, tree_values[b])
        mixed = mixed.reshape(part_requests, heads, BRANCH, HD)
        for h in range(heads):
            att[i, d, :, h * HD : (h + 1) * HD] = mixed[:, h].reshape(own, HD).astype(jnp.bfloat16)
        for k in range(m - 1):
            att_copy(i, k).start()

        @pl.when(i > 0)
        def _():
            finish(i - 1)

        @pl.when(gathering)
        def _():
            product(later, t, True)

        for k in range(m - 1):
            att_copy(i, k).wait_recv()

        @pl.when(i == 0)
        def _():
            for load in loads[4:]:
                load.wait()

        attended = att[i].reshape(rows, head_cols)
        for u in range(SUBS):
            done = set()
            for k in range(n):
                right, left = n - 1 - k, k
                for s in (right, left):
                    if s not in done:
                        low = s * share + u * sub
                        part[s, u] = dot32(attended, wo[:, low : low + sub])
                        done.add(s)
                if k < n - 1:

                    @pl.when(t == 0)
                    def _():
                        rs_send[i, right, u] = part[right, u].astype(jnp.bfloat16)
                        rs_right(i, right, u).start()

                    @pl.when(t == n - 1)
                    def _():
                        rs_send[i, left, u] = part[left, u].astype(jnp.bfloat16)
                        rs_left(i, left, u).start()

        if n > 2:

            @pl.when(gathering)
            def _():
                gather_wave(later, 1)

            sum_wave(i, 1, 0)

            @pl.when(gathering)
            def _():
                for k in range(2, n - 1):
                    gather_wave(later, k)

        return carry

    lax.fori_loop(0, steps, step, 0)
    later_waves(steps - 1)
    finish(steps - 1)

    def drain(i, carry):
        for k in range(m - 1):
            proj_copy(i, k).wait_send()
            dsum_copy(i, k).wait_send()
            att_copy(i, k).wait_send()
        for u in range(SUBS):
            for s in range(n):

                @pl.when(t < s)
                def _():
                    rs_right(i, s, u).wait_send()

                @pl.when(t > s)
                def _():
                    rs_left(i, s, u).wait_send()

        @pl.when(i >= BATCHES)
        def _():
            for k in range(n - 1):
                tsum_copy(i, k).wait_send()
            for u in range(SUBS):
                for s in range(n):

                    @pl.when((s <= t) & (t < n - 1))
                    def _():
                        ag_copy(i, s, u, t + 1, s).wait_send()

                    @pl.when((s > t) & (t > 0))
                    def _():
                        ag_copy(i, s, u, t - 1, s).wait_send()

                @pl.when(t > 0)
                def _():
                    ag_copy(i, t, u, t - 1, n).wait_send()

        return carry

    lax.fori_loop(0, steps, drain, 0)


def kernel_shards(
    root_features,
    branch_embeds,
    parents,
    cache_lengths,
    cache_kv,
    norm_gain,
    w_query,
    w_keyval,
    w_out,
):
    n = lax.axis_size("tensor")
    m = lax.axis_size("dp")
    requests, feat = root_features.shape
    own_requests = cache_lengths.shape[0]
    part_requests = own_requests // BATCHES
    own = part_requests * BRANCH
    rows = own * m
    lanes = -(-rows // 128) * 128
    steps = BATCHES * DEPTHS
    share = feat // n
    head_cols = w_query.shape[1]
    proj_cols = head_cols + 2 * HD

    def one_hots(table):
        count = rows
        split = table.reshape(m, BATCHES, part_requests, DEPTHS - 1, BRANCH)
        split = jnp.transpose(split, (3, 1, 0, 2, 4)).reshape((DEPTHS - 1) * BATCHES, count)
        lane = jnp.arange(count, dtype=jnp.int32)
        index = split + (lane // BRANCH * BRANCH)[None, :]
        return (index[:, :, None] == lane[None, None, :]).astype(jnp.bfloat16)

    hot = one_hots(parents)
    bf16, f32 = jnp.bfloat16, jnp.float32
    vmem = pl.BlockSpec(memory_space=pltpu.VMEM)
    smem = pl.BlockSpec(memory_space=pltpu.SMEM)
    hbm = pl.BlockSpec(memory_space=pl.ANY)
    dma = pltpu.SemaphoreType.DMA
    return pl.pallas_call(
        functools.partial(tree_kernel, n, m),
        out_shape=jax.ShapeDtypeStruct((requests, DEPTHS, BRANCH, share), bf16),
        in_specs=[vmem, hbm, vmem, smem, hbm, vmem, hbm, hbm, hbm],
        out_specs=vmem,
        scratch_shapes=[
            pltpu.VMEM((requests, BRANCH, feat), bf16),
            pltpu.VMEM((DEPTHS - 1, requests, BRANCH, share), bf16),
            pltpu.VMEM(cache_kv.shape, bf16),
            pltpu.VMEM((feat, head_cols), bf16),
            pltpu.VMEM((feat, 2 * HD), bf16),
            pltpu.VMEM((head_cols, feat), bf16),
            pltpu.VMEM((steps, n, SUBS, rows, share // SUBS), bf16),
            pltpu.VMEM((steps, n, 8, lanes), f32),
            pltpu.VMEM((BATCHES, SUBS, rows, share // SUBS), f32),
            pltpu.VMEM((rows, proj_cols), f32),
            pltpu.VMEM((steps, m, own, proj_cols), bf16),
            pltpu.VMEM((steps, m - 1, own, proj_cols), bf16),
            pltpu.VMEM((steps, 8, lanes), f32),
            pltpu.VMEM((steps, m - 1, 8, lanes), f32),
            pltpu.VMEM((BATCHES, DEPTHS * own, HD), bf16),
            pltpu.VMEM((BATCHES, DEPTHS * own, HD), bf16),
            pltpu.VMEM((BATCHES, rows, DEPTHS * own), bf16),
            pltpu.VMEM((steps, m, own, head_cols), bf16),
            pltpu.VMEM((n, SUBS, rows, share // SUBS), f32),
            pltpu.VMEM((steps, n, SUBS, rows, share // SUBS), bf16),
            pltpu.VMEM((steps, n + 1, SUBS, rows, share // SUBS), bf16),
            pltpu.VMEM((SUBS, rows, share // SUBS), f32),
            dma((4 + DEPTHS,)),
            dma((steps, n + 1, SUBS)),
            dma((steps, n, SUBS)),
            dma((steps, n - 1)),
            dma((steps, n - 1)),
            dma((steps, m - 1)),
            dma((steps, m - 1)),
            dma((steps, m - 1)),
            dma((steps, m - 1)),
            dma((steps, m - 1)),
            dma((steps, m - 1)),
            dma((steps, n, SUBS)),
            dma((steps, n + 1, SUBS)),
        ],
        compiler_params=pltpu.CompilerParams(
            collective_id=0, has_side_effects=True, vmem_limit_bytes=60 * 1024 * 1024
        ),
    )(
        root_features,
        branch_embeds,
        hot,
        cache_lengths,
        cache_kv,
        norm_gain[None, :],
        w_query,
        w_keyval.reshape(feat, 2 * HD),
        w_out,
    )


def solution(mesh):
    in_line = 1 < mesh.shape["tensor"] <= 8 and mesh.shape["dp"] > 1
    return jax.shard_map(
        kernel_shards if in_line else shards,
        mesh=mesh,
        in_specs=(
            P("groups", "dp"),
            P("groups", None, None, "dp"),
            P("groups", None, None),
            P(("groups", "dp")),
            P(("groups", "dp"), None, None, "tensor"),
            P("dp"),
            P("dp", "tensor"),
            P("dp", None, "tensor"),
            P("tensor", "dp"),
        ),
        out_specs=P("groups", None, None, ("dp", "tensor")),
        check_vma=False,
    )
```
